32 devices in a mesh: groups: 2 (over y), blk: 4 (over z), kv: 2 (over x), pair: 2 (over core).
Axes of the slice: x: 2, y: 2, z: 4, core: 2. Of those that a mesh axis runs over, the one named last changes fastest.
Arguments:
- queries: bfloat16 [128, 128, 128], P(('groups', 'blk'), ('kv', 'pair')), parts along dimension 0, may hold values from -15 to 15
- root_keys: bfloat16 [16384, 8, 128], P(('groups', 'blk', 'pair'), 'kv'), parts along dimension 0, may hold values from -4 to 4
- root_values: bfloat16 [16384, 8, 128], P(('groups', 'blk', 'pair'), 'kv'), parts along dimension 0, may hold values from -6 to 6
- branch_keys: bfloat16 [16, 2048, 8, 128], P(('groups', 'blk'), 'pair', 'kv'), parts along dimension 0, may hold values from -4 to 4
- branch_values: bfloat16 [16, 2048, 8, 128], P(('groups', 'blk'), 'pair', 'kv'), parts along dimension 0, may hold values from -6 to 6
- request_branch: int32 [128], P(('groups', 'blk')), parts along dimension 0, may hold values from 0 to 7, as said below
- seen_tokens: int32 [128], P(('groups', 'blk')), parts along dimension 0, may hold values from 1 to 2048, as said below
Outputs:
- attended: bfloat16 [128, 128, 128], P(('groups', 'blk'), ('kv', 'pair')), parts along dimension 0
The draws below stay inside these ranges and needn't reach their ends.
There are 2 independent parts, one for each index of `groups`. The reference program is written for one: setup_inputs(seed, part) draws one part's arguments, and reference() takes and returns one part's arrays. A program takes and returns all parts, laid end to end along the dimension named above; each array names one. Nothing has to cross between parts.
Inputs may be any that keep to these rules, and one draw needn't show every extreme that they name: Within a part, request r belongs to one of the 2 branches stored on its own index of blk: request_branch[r] // 2 == r // 16, with r and the branch counted within the part. Every branch has at least one request. `seen_tokens`: on every index of blk some request sees all 2048 positions of its branch.
All inputs are finite; a program needn't handle non-finite values.
Results may differ from the reference program's by a relative error of at most 0.04.
Values may be sent and summed in bfloat16 or wider, within the bound.
A program may use at most 64 MiB of HBM per device.

```python
import jax
import jax.numpy as jnp
from jax import lax

H = 128
KVH = 8
HD = 128
REQ_DEV = 16
BR_DEV = 2
REQ = 64
BRANCHES = 8
ROOT = 8192
BLEN = 2048


def draw_queries(key, part):
    result = 3.0 * jax.random.truncated_normal(key, -5.0, 5.0, (REQ, H, HD), jnp.float32)
    return result.astype(jnp.bfloat16)


def draw_root_keys(key, part):
    draw_key = jax.random.fold_in(key, 31)
    result = jax.random.truncated_normal(draw_key, -4.0, 4.0, (ROOT, KVH, HD), jnp.float32)
    return result.astype(jnp.bfloat16)


def draw_branch_keys(key, part):
    draw_key = jax.random.fold_in(key, 37)
    result = jax.random.truncated_normal(draw_key, -4.0, 4.0, (BRANCHES, BLEN, KVH, HD), jnp.float32)
    return result.astype(jnp.bfloat16)


def shuffled_slots(key, blocks):
    seeds = jax.random.split(key, blocks)
    return jax.vmap(lambda seed_key: jax.random.permutation(seed_key, REQ_DEV))(seeds)


def draw_request_branch(key, part):
    blocks = REQ // REQ_DEV
    order = shuffled_slots(jax.random.fold_in(key, 11), blocks)
    extra = jax.random.randint(jax.random.fold_in(key, 12), (blocks, REQ_DEV), 0, BR_DEV)
    local = jnp.where(order < BR_DEV, order, extra)
    return (local + BR_DEV * jnp.arange(blocks)[:, None]).reshape(REQ).astype(jnp.int32)


def draw_seen_tokens(key, part):
    blocks = REQ // REQ_DEV
    order = shuffled_slots(jax.random.fold_in(key, 21), blocks)
    lengths = jax.random.randint(jax.random.fold_in(key, 22), (blocks, REQ_DEV), 1, BLEN + 1)
    return jnp.where(order == 0, BLEN, lengths).reshape(REQ).astype(jnp.int32)


def levels(stream_key, shape, cuts, low, top_value):
    loudness, own = 1.0, jax.random.fold_in(stream_key, 6)
    for axis_at, shards_of in cuts:
        draws = jnp.exp(jax.random.uniform(jax.random.fold_in(own, axis_at), (shards_of,), jnp.float32, low / len(cuts), top_value / len(cuts)))
        loudness = loudness * jnp.repeat(draws, shape[axis_at] // shards_of).reshape([-1 if axis == axis_at else 1 for axis in range(len(shape))])
    return loudness


def noise(rng, extent, scale, most, shards=(), held_as=jnp.bfloat16):
    level = levels(rng, extent, shards, -0.22, 0.18) if shards else 1.0
    entries = jax.random.normal(rng, extent, jnp.float32) * scale * level
    return jnp.minimum(jnp.maximum(entries, -most), most).astype(held_as)


def setup_inputs(seed: int = 0, part: int = 0) -> dict:
    splits = jax.random.split(jax.random.key(seed), 8)
    own_keys = jax.random.split(jax.random.fold_in(splits[7], part), 8)
    queries = draw_queries(jax.random.fold_in(jax.random.fold_in(splits[7], part), 71), part)
    root_keys = draw_root_keys(jax.random.fold_in(jax.random.fold_in(splits[7], part), 71), part)
    root_values = noise(own_keys[2], (ROOT, KVH, HD), 1.0, 6.0, ((0, 8), (1, 2)))
    branch_keys = draw_branch_keys(jax.random.fold_in(jax.random.fold_in(splits[7], part), 71), part)
    branch_values = noise(own_keys[4], (BRANCHES, BLEN, KVH, HD), 1.0, 6.0, ((0, 4), (1, 2), (2, 2)))
    request_branch = draw_request_branch(jax.random.fold_in(jax.random.fold_in(splits[7], part), 71), part)
    seen_tokens = draw_seen_tokens(jax.random.fold_in(jax.random.fold_in(splits[7], part), 71), part)
    return {"queries": queries, "root_keys": root_keys, "root_values": root_values, "branch_keys": branch_keys, "branch_values": branch_values, "request_branch": request_branch, "seen_tokens": seen_tokens}


def reference(queries, root_keys, root_values, branch_keys, branch_values, request_branch, seen_tokens):
    group_size = H // KVH
    score_scale = 1.0 / (HD ** 0.5)
    keys_wide = root_keys.astype(jnp.float32)
    values_wide = root_values.astype(jnp.float32)
    positions = jnp.arange(BLEN, dtype=jnp.int32)

    def one_request(request_items):
        query_row, branch_id, seen_count = request_items
        query_heads = query_row.astype(jnp.float32).reshape(KVH, group_size, HD)
        keys_own = lax.dynamic_index_in_dim(branch_keys, branch_id.astype(jnp.int32), 0, keepdims=False).astype(jnp.float32)
        values_own = lax.dynamic_index_in_dim(branch_values, branch_id.astype(jnp.int32), 0, keepdims=False).astype(jnp.float32)
        scores_root = jnp.einsum("kgd,tkd->kgt", query_heads, keys_wide) * score_scale
        scores_branch = jnp.einsum("kgd,tkd->kgt", query_heads, keys_own) * score_scale
        visible = positions < seen_count
        scores_branch = jnp.where(visible, scores_branch, -1.0e30)
        largest = jnp.maximum(jnp.max(scores_root, axis=-1), jnp.max(scores_branch, axis=-1))
        weights_root = jnp.exp(scores_root - largest[..., None])
        weights_branch = jnp.where(visible, jnp.exp(scores_branch - largest[..., None]), 0.0)
        totals = jnp.sum(weights_root, axis=-1) + jnp.sum(weights_branch, axis=-1)
        rounded_root = lax.optimization_barrier(weights_root.astype(jnp.bfloat16)).astype(jnp.float32)
        rounded_branch = lax.optimization_barrier(weights_branch.astype(jnp.bfloat16)).astype(jnp.float32)
        weighted = jnp.einsum("kgt,tkd->kgd", rounded_root, values_wide)
        weighted = weighted + jnp.einsum("kgt,tkd->kgd", rounded_branch, values_own)
        return (weighted / totals[..., None]).astype(jnp.bfloat16).reshape(H, HD)

    return lax.map(one_request, (queries, request_branch, seen_tokens))
```

```python
import functools
import math

import jax
import jax.numpy as jnp
from jax import lax
from jax.experimental import pallas as pl
from jax.experimental.pallas import tpu as pltpu
from jax.sharding import PartitionSpec as P

MESH = pl.DeviceIdType.MESH
masked_floor = -1e30
log2e = 1.4426950408889634


def kernel(
    blocks, branches,
    q_ref, rk_ref, rv_ref, bk_ref, bv_ref, rb_ref, seen_ref,
    out_ref,
    in_r, in_b, stage, mine_r, mine_b, give_r, give_b,
    q_all, p_send, p_recv, s_send, s_recv, acc_ref, max_ref, tot_ref,
    load_sem, kv_send, kv_recv, q_send, q_recv, ps_sem, pr_sem, ss_sem, sr_sem,
):
    requests, heads, width = q_ref.shape
    half = mine_r.shape[1]
    shared = 2 * half
    group = heads // half
    rows = requests * group
    root_tokens = give_r.shape[2]
    branch_tokens = give_b.shape[2]
    per_branch = branch_tokens // branches
    factor = log2e / math.sqrt(width)
    me = lax.axis_index("blk")
    core = lax.axis_index("pair")
    other = 1 - core

    loads = []
    for at, (src, dst) in enumerate(
        ((rk_ref, in_r.at[0]), (rv_ref, in_r.at[1]), (bk_ref, in_b.at[0]), (bv_ref, in_b.at[1]))
    ):
        copy = pltpu.make_async_copy(src, dst, load_sem.at[at])
        copy.start()
        loads.append(copy)

    barrier = pltpu.get_barrier_semaphore()

    @pl.loop(1, blocks)
    def _(apart):
        pl.semaphore_signal(
            barrier, inc=1, device_id={"blk": lax.rem(me + apart, blocks)}, device_id_type=MESH
        )

    pl.semaphore_signal(barrier, inc=1, device_id={"pair": other}, device_id_type=MESH)
    pl.semaphore_wait(barrier, blocks)

    def q_part(ref, i):
        return ref.at[:, pl.ds(i * group, group), :]

    def q_copy(src, slot, i, side, target):
        return pltpu.make_async_remote_copy(
            src_ref=src,
            dst_ref=q_part(q_all.at[slot], i),
            send_sem=q_send.at[side, slot, i],
            recv_sem=q_recv.at[slot, i],
            device_id={"blk": target},
            device_id_type=MESH,
        )

    for i in range(half):
        @pl.when(me + 1 < blocks)
        def _():
            q_copy(q_part(q_ref, i), me, i, 0, me + 1).start()

        @pl.when(me >= 1)
        def _():
            q_copy(q_part(q_ref, i), me, i, 1, me - 1).start()

    def forward(step):
        for i in range(half):
            @pl.when(me - step >= 0)
            def _():
                slot = me - step
                q_copy(q_part(q_ref, i), slot, i, 0, me).wait_recv()

                @pl.when(me + 1 < blocks)
                def _():
                    q_copy(q_part(q_all.at[slot], i), slot, i, 0, me + 1).start()

            @pl.when(me + step < blocks)
            def _():
                slot = me + step
                q_copy(q_part(q_ref, i), slot, i, 1, me).wait_recv()

                @pl.when(me >= 1)
                def _():
                    q_copy(q_part(q_all.at[slot], i), slot, i, 1, me - 1).start()

    def kv_copy(at, give, mine, kind, tokens):
        return pltpu.make_async_remote_copy(
            src_ref=give.at[kind],
            dst_ref=mine.at[kind, :, pl.ds(tokens, tokens), :],
            send_sem=kv_send.at[at],
            recv_sem=kv_recv.at[at],
            device_id={"pair": other},
            device_id_type=MESH,
        )

    kv_copies = (
        kv_copy(0, give_r, mine_r, 0, root_tokens),
        kv_copy(1, give_r, mine_r, 1, root_tokens),
        kv_copy(2, give_b, mine_b, 0, branch_tokens),
        kv_copy(3, give_b, mine_b, 1, branch_tokens),
    )
    span = stage.shape[0] // shared

    def spread(src, kind, mine, give, tokens):
        @pl.loop(0, tokens // span)
        def _(chunk):
            first = pl.multiple_of(chunk * (span * shared), span * shared)
            stage[...] = src[kind, pl.ds(first, span * shared), :].astype(jnp.float32)
            at = pl.multiple_of(chunk * span, span)
            for i in range(half):
                give[kind, i, pl.ds(at, span), :] = stage[
                    pl.ds(other * half + i, span, stride=shared), :
                ].astype(jnp.bfloat16)
                mine[kind, i, pl.ds(at, span), :] = stage[
                    pl.ds(core * half + i, span, stride=shared), :
                ].astype(jnp.bfloat16)

    for kind in range(2):
        loads[kind].wait()
        spread(in_r, kind, mine_r, give_r, root_tokens)
        kv_copies[kind].start()
    forward(1)
    for kind in range(2):
        loads[2 + kind].wait()
        spread(in_b, kind, mine_b, give_b, branch_tokens)
        kv_copies[2 + kind].start()

    def attend(query, keys, values, ranges):
        scores = lax.dot_general(
            query, keys, (((1,), (1,)), ((), ())), preferred_element_type=jnp.float32
        )
        if ranges is not None:
            column = lax.broadcasted_iota(jnp.int32, (group, scores.shape[1]), 1)
            visible = [(column >= low) & (column < high) for low, high in ranges]
            scores = jnp.concatenate(
                [
                    jnp.where(seen, scores[r * group : (r + 1) * group], masked_floor)
                    for r, seen in enumerate(visible)
                ],
                axis=0,
            )
        largest = jnp.max(scores, axis=-1, keepdims=True)
        weights = jnp.exp2((scores - largest) * factor)
        if ranges is not None:
            weights = jnp.where(scores > 0.5 * masked_floor, weights, 0.0)
        totals = jnp.sum(weights, axis=-1, keepdims=True)
        sums = jnp.dot(weights.astype(jnp.bfloat16), values, preferred_element_type=jnp.float32)
        return sums, largest * factor, totals

    def p_copies(slot, i, target):
        place = pl.ds(i * rows, rows)
        return (
            pltpu.make_async_remote_copy(
                src_ref=p_send.at[slot, place, :],
                dst_ref=p_recv.at[target, place, :],
                send_sem=ps_sem.at[slot, i],
                recv_sem=pr_sem.at[target, i],
                device_id={"blk": slot},
                device_id_type=MESH,
            ),
            pltpu.make_async_remote_copy(
                src_ref=s_send.at[slot, i],
                dst_ref=s_recv.at[target, i],
                send_sem=ss_sem.at[slot, i],
                recv_sem=sr_sem.at[target, i],
                device_id={"blk": slot},
                device_id_type=MESH,
            ),
        )

    kv_copies[0].wait_recv()
    kv_copies[1].wait_recv()

    @pl.loop(1, blocks)
    def _(step):
        @pl.when(step >= 2)
        def _():
            forward(step)

        @pl.loop(0, 2)
        def _(side):
            slot = me + step * (2 * side - 1)

            @pl.when((slot >= 0) & (slot < blocks))
            def _():
                for i in range(half):
                    query = q_all[slot, :, i * group : (i + 1) * group, :].reshape(rows, width)
                    sums, largest, totals = attend(query, mine_r[0, i], mine_r[1, i], None)
                    p_send[slot, i * rows : (i + 1) * rows, :] = (sums / totals).astype(
                        jnp.bfloat16
                    )
                    level = jnp.broadcast_to(largest + jnp.log(totals) * log2e, (rows, 128))
                    s_send[slot, i] = level.T[0:1, :]
                    for copy in p_copies(slot, i, me):
                        copy.start()

    kv_copies[2].wait_recv()
    kv_copies[3].wait_recv()
    ranges = ([], [])
    for r in range(requests):
        start = lax.rem(rb_ref[r], branches) * per_branch
        seen = seen_ref[r]
        for piece, owner in enumerate((core, other)):
            length = jnp.clip(seen - owner * per_branch, 0, per_branch)
            ranges[piece].append((start, start + length))
    for i in range(half):
        query = q_ref[:, i * group : (i + 1) * group, :].reshape(rows, width)
        sums, largest, totals = attend(query, mine_r[0, i], mine_r[1, i], None)
        for piece in range(2):
            place = slice(piece * branch_tokens, (piece + 1) * branch_tokens)
            more = attend(query, mine_b[0, i, place, :], mine_b[1, i, place, :], ranges[piece])
            joint = jnp.maximum(largest, more[1])
            one, two = jnp.exp2(largest - joint), jnp.exp2(more[1] - joint)
            sums = sums * one + more[0] * two
            totals = totals * one + more[2] * two
            largest = joint
        acc_ref[i] = sums
        max_ref[i] = jnp.broadcast_to(largest, (rows, width))
        tot_ref[i] = jnp.broadcast_to(totals, (rows, width))

    @pl.loop(1, blocks)
    def _(step):
        @pl.loop(0, 2)
        def _(side):
            slot = me + step * (2 * side - 1)

            @pl.when((slot >= 0) & (slot < blocks))
            def _():
                for i in range(half):
                    for copy in p_copies(slot, i, slot):
                        copy.wait_recv()
                    level = jnp.broadcast_to(s_recv[slot, i], (128, rows)).T
                    joint = jnp.maximum(max_ref[i], level)
                    one, two = jnp.exp2(max_ref[i] - joint), jnp.exp2(level - joint)
                    part = p_recv[slot, i * rows : (i + 1) * rows, :].astype(jnp.float32)
                    acc_ref[i] = acc_ref[i] * one + part * two
                    tot_ref[i] = tot_ref[i] * one + two
                    max_ref[i] = joint

    for i in range(half):
        out_ref[:, i * group : (i + 1) * group, :] = (
            (acc_ref[i] / tot_ref[i]).astype(jnp.bfloat16).reshape(requests, group, width)
        )

    for copy in kv_copies:
        copy.wait_send()

    for i in range(half):
        @pl.when(me + 1 < blocks)
        def _():
            q_copy(q_part(q_ref, i), me, i, 0, me + 1).wait_send()

        @pl.when(me >= 1)
        def _():
            q_copy(q_part(q_ref, i), me, i, 1, me - 1).wait_send()

    @pl.loop(1, blocks)
    def _(step):
        for i in range(half):
            @pl.when((me - step >= 0) & (me + 1 < blocks))
            def _():
                slot = me - step
                q_copy(q_part(q_all.at[slot], i), slot, i, 0, me + 1).wait_send()

            @pl.when((me + step < blocks) & (me >= 1))
            def _():
                slot = me + step
                q_copy(q_part(q_all.at[slot], i), slot, i, 1, me - 1).wait_send()

        slot = lax.rem(me + step, blocks)
        for i in range(half):
            for copy in p_copies(slot, i, me):
                copy.wait_send()


def local(queries, root_keys, root_values, branch_keys, branch_values, request_branch, seen_tokens):
    requests, heads, width = queries.shape
    root_tokens, shared, _ = root_keys.shape
    branches, per_branch, _, _ = branch_keys.shape
    branch_tokens = branches * per_branch
    blocks = lax.axis_size("blk")
    half = shared // lax.axis_size("pair")
    rows = requests * (heads // half)
    span = min(512, root_tokens, branch_tokens)
    bf16, f32 = jnp.bfloat16, jnp.float32
    dma = pltpu.SemaphoreType.DMA
    return pl.pallas_call(
        functools.partial(kernel, blocks, branches),
        out_shape=jax.ShapeDtypeStruct(queries.shape, bf16),
        in_specs=[pl.BlockSpec(memory_space=pltpu.VMEM)]
        + [pl.BlockSpec(memory_space=pl.ANY)] * 4
        + [pl.BlockSpec(memory_space=pltpu.SMEM)] * 2,
        out_specs=pl.BlockSpec(memory_space=pltpu.VMEM),
        scratch_shapes=[
            pltpu.VMEM((2, root_tokens * shared, width), bf16),
            pltpu.VMEM((2, branch_tokens * shared, width), bf16),
            pltpu.VMEM((span * shared, width), f32),
            pltpu.VMEM((2, half, 2 * root_tokens, width), bf16),
            pltpu.VMEM((2, half, 2 * branch_tokens, width), bf16),
            pltpu.VMEM((2, half, root_tokens, width), bf16),
            pltpu.VMEM((2, half, branch_tokens, width), bf16),
            pltpu.VMEM((blocks, requests, heads, width), bf16),
            pltpu.VMEM((blocks, half * rows, width), bf16),
            pltpu.VMEM((blocks, half * rows, width), bf16),
            pltpu.VMEM((blocks, half, 1, rows), f32),
            pltpu.VMEM((blocks, half, 1, rows), f32),
            pltpu.VMEM((half, rows, width), f32),
            pltpu.VMEM((half, rows, width), f32),
            pltpu.VMEM((half, rows, width), f32),
            dma((4,)),
            dma((4,)),
            dma((4,)),
            dma((2, blocks, half)),
            dma((blocks, half)),
            dma((blocks, half)),
            dma((blocks, half)),
            dma((blocks, half)),
            dma((blocks, half)),
        ],
        compiler_params=pltpu.CompilerParams(collective_id=0, has_side_effects=True),
        name="tree_attention",
    )(
        queries,
        root_keys.reshape(root_tokens * shared, width),
        root_values.reshape(root_tokens * shared, width),
        branch_keys.reshape(branch_tokens * shared, width),
        branch_values.reshape(branch_tokens * shared, width),
        request_branch,
        seen_tokens,
    )


def solution(mesh):
    in_specs = (
        P(("groups", "blk"), ("kv", "pair"), None),
        P(("groups", "blk", "pair"), "kv", None),
        P(("groups", "blk", "pair"), "kv", None),
        P(("groups", "blk"), "pair", "kv", None),
        P(("groups", "blk"), "pair", "kv", None),
        P(("groups", "blk")),
        P(("groups", "blk")),
    )
    out_specs = P(("groups", "blk"), ("kv", "pair"), None)
    return jax.shard_map(local, mesh=mesh, in_specs=in_specs, out_specs=out_specs, check_vma=False)
```

```python
import functools
import math

import jax
import jax.numpy as jnp
from jax import lax
from jax.experimental import pallas as pl
from jax.experimental.pallas import tpu as pltpu
from jax.sharding import PartitionSpec as P

MESH = pl.DeviceIdType.MESH
masked_floor = -1e30
log2e = 1.4426950408889634


def kernel(
    blocks, branches,
    q_ref, rk_ref, rv_ref, bk_ref, bv_ref, rb_ref, seen_ref,
    out_ref,
    in_r, in_b, stage, mine_r, mine_b, give_r, give_b,
    q_all, p_send, p_recv, s_send, s_recv, acc_ref, max_ref, tot_ref,
    load_sem, kv_send, kv_recv, q_send, q_recv, ps_sem, pr_sem, ss_sem, sr_sem,
):
    requests, heads, width = q_ref.shape
    half = mine_r.shape[1]
    shared = 2 * half
    group = heads // half
    rows = requests * group
    root_tokens = give_r.shape[2]
    branch_tokens = give_b.shape[2]
    per_branch = branch_tokens // branches
    factor = log2e / math.sqrt(width)
    me = lax.axis_index("blk")
    core = lax.axis_index("pair")
    other = 1 - core

    loads = []
    for at, (src, dst) in enumerate(
        ((rk_ref, in_r.at[0]), (rv_ref, in_r.at[1]), (bk_ref, in_b.at[0]), (bv_ref, in_b.at[1]))
    ):
        copy = pltpu.make_async_copy(src, dst, load_sem.at[at])
        copy.start()
        loads.append(copy)

    barrier = pltpu.get_barrier_semaphore()

    for near in (me - 1, me + 1):
        @pl.when((near >= 0) & (near < blocks))
        def _():
            pl.semaphore_signal(barrier, inc=1, device_id={"blk": near}, device_id_type=MESH)

    pl.semaphore_signal(barrier, inc=1, device_id={"pair": other}, device_id_type=MESH)

    def q_part(ref, i):
        return ref.at[:, pl.ds(i * group, group), :]

    def q_copy(src, slot, i, side, target):
        return pltpu.make_async_remote_copy(
            src_ref=src,
            dst_ref=q_part(q_all.at[slot], i),
            send_sem=q_send.at[side, slot, i],
            recv_sem=q_recv.at[slot, i],
            device_id={"blk": target},
            device_id_type=MESH,
        )

    def forward(step):
        for i in range(half):
            @pl.when((me - step >= 0) & (me + 1 < blocks))
            def _():
                slot = me - step
                q_copy(q_part(q_ref, i), slot, i, 0, me).wait_recv()
                q_copy(q_part(q_all.at[slot], i), slot, i, 0, me + 1).start()

            @pl.when((me + step < blocks) & (me >= 1))
            def _():
                slot = me + step
                q_copy(q_part(q_ref, i), slot, i, 1, me).wait_recv()
                q_copy(q_part(q_all.at[slot], i), slot, i, 1, me - 1).start()

    def kv_copy(at, give, mine, kind, tokens):
        return pltpu.make_async_remote_copy(
            src_ref=give.at[kind],
            dst_ref=mine.at[kind, :, pl.ds(tokens, tokens), :],
            send_sem=kv_send.at[at],
            recv_sem=kv_recv.at[at],
            device_id={"pair": other},
            device_id_type=MESH,
        )

    kv_copies = (
        kv_copy(0, give_r, mine_r, 0, root_tokens),
        kv_copy(1, give_r, mine_r, 1, root_tokens),
        kv_copy(2, give_b, mine_b, 0, branch_tokens),
        kv_copy(3, give_b, mine_b, 1, branch_tokens),
    )
    span = stage.shape[0] // shared

    def spread(src, kind, mine, give, tokens):
        @pl.loop(0, tokens // span)
        def _(chunk):
            first = pl.multiple_of(chunk * (span * shared), span * shared)
            stage[...] = src[kind, pl.ds(first, span * shared), :].astype(jnp.float32)
            at = pl.multiple_of(chunk * span, span)
            for i in range(half):
                give[kind, i, pl.ds(at, span), :] = stage[
                    pl.ds(other * half + i, span, stride=shared), :
                ].astype(jnp.bfloat16)
                mine[kind, i, pl.ds(at, span), :] = stage[
                    pl.ds(core * half + i, span, stride=shared), :
                ].astype(jnp.bfloat16)

    @pl.when((me >= 1) & (me + 1 < blocks))
    def _():
        pl.semaphore_wait(barrier, 3)

    @pl.when((me < 1) | (me + 1 >= blocks))
    def _():
        pl.semaphore_wait(barrier, 2)

    for i in range(half):
        @pl.when(me + 1 < blocks)
        def _():
            q_copy(q_part(q_ref, i), me, i, 0, me + 1).start()

        @pl.when(me >= 1)
        def _():
            q_copy(q_part(q_ref, i), me, i, 1, me - 1).start()

    for kind in range(2):
        loads[kind].wait()
        spread(in_r, kind, mine_r, give_r, root_tokens)

    for kind in range(2):
        kv_copies[kind].start()
    for kind in range(2):
        loads[2 + kind].wait()
        spread(in_b, kind, mine_b, give_b, branch_tokens)
        kv_copies[2 + kind].start()
    forward(1)

    def attend(query, keys, values, ranges):
        scores = lax.dot_general(
            query, keys, (((1,), (1,)), ((), ())), preferred_element_type=jnp.float32
        )
        if ranges is not None:
            column = lax.broadcasted_iota(jnp.int32, (group, scores.shape[1]), 1)
            visible = [(column >= low) & (column < high) for low, high in ranges]
            scores = jnp.concatenate(
                [
                    jnp.where(seen, scores[r * group : (r + 1) * group], masked_floor)
                    for r, seen in enumerate(visible)
                ],
                axis=0,
            )
        largest = jnp.max(scores, axis=-1, keepdims=True)
        weights = jnp.exp2((scores - largest) * factor)
        if ranges is not None:
            weights = jnp.where(scores > 0.5 * masked_floor, weights, 0.0)
        totals = jnp.sum(weights, axis=-1, keepdims=True)
        sums = jnp.dot(weights.astype(jnp.bfloat16), values, preferred_element_type=jnp.float32)
        return sums, largest * factor, totals

    def p_copies(slot, i, target):
        place = pl.ds(i * rows, rows)
        return (
            pltpu.make_async_remote_copy(
                src_ref=p_send.at[slot, place, :],
                dst_ref=p_recv.at[target, place, :],
                send_sem=ps_sem.at[slot, i],
                recv_sem=pr_sem.at[target, i],
                device_id={"blk": slot},
                device_id_type=MESH,
            ),
            pltpu.make_async_remote_copy(
                src_ref=s_send.at[slot, i],
                dst_ref=s_recv.at[target, i],
                send_sem=ss_sem.at[slot, i],
                recv_sem=sr_sem.at[target, i],
                device_id={"blk": slot},
                device_id_type=MESH,
            ),
        )

    kv_copies[0].wait_recv()
    kv_copies[1].wait_recv()

    @pl.loop(1, blocks)
    def _(step):
        @pl.loop(0, 2)
        def _(side):
            slot = me + step * (2 * side - 1)
            after = me + 1 - 2 * side

            @pl.when((side == 1) & (step + 1 < blocks))
            def _():
                forward(step + 1)

            @pl.when((slot >= 0) & (slot < blocks))
            def _():
                for i in range(half):
                    @pl.when((after < 0) | (after >= blocks))
                    def _():
                        q_copy(q_part(q_ref, i), slot, i, 0, me).wait_recv()

                    query = q_all[slot, :, i * group : (i + 1) * group, :].reshape(rows, width)
                    sums, largest, totals = attend(query, mine_r[0, i], mine_r[1, i], None)
                    p_send[slot, i * rows : (i + 1) * rows, :] = (sums / totals).astype(
                        jnp.bfloat16
                    )
                    level = jnp.broadcast_to(largest + jnp.log(totals) * log2e, (rows, 128))
                    s_send[slot, i] = level.T[0:1, :]
                    for copy in p_copies(slot, i, me):
                        copy.start()

    kv_copies[2].wait_recv()
    kv_copies[3].wait_recv()
    ranges = ([], [])
    for r in range(requests):
        start = lax.rem(rb_ref[r], branches) * per_branch
        seen = seen_ref[r]
        for piece, owner in enumerate((core, other)):
            length = jnp.clip(seen - owner * per_branch, 0, per_branch)
            ranges[piece].append((start, start + length))
    for i in range(half):
        query = q_ref[:, i * group : (i + 1) * group, :].reshape(rows, width)
        sums, largest, totals = attend(query, mine_r[0, i], mine_r[1, i], None)
        for piece in range(2):
            place = slice(piece * branch_tokens, (piece + 1) * branch_tokens)
            more = attend(query, mine_b[0, i, place, :], mine_b[1, i, place, :], ranges[piece])
            joint = jnp.maximum(largest, more[1])
            one, two = jnp.exp2(largest - joint), jnp.exp2(more[1] - joint)
            sums = sums * one + more[0] * two
            totals = totals * one + more[2] * two
            largest = joint
        acc_ref[i] = sums
        max_ref[i] = jnp.broadcast_to(largest, (rows, width))
        tot_ref[i] = jnp.broadcast_to(totals, (rows, width))

    @pl.loop(1, blocks)
    def _(step):
        @pl.loop(0, 2)
        def _(side):
            slot = me + step * (2 * side - 1)

            @pl.when((slot >= 0) & (slot < blocks))
            def _():
                for i in range(half):
                    for copy in p_copies(slot, i, slot):
                        copy.wait_recv()
                    level = jnp.broadcast_to(s_recv[slot, i], (128, rows)).T
                    joint = jnp.maximum(max_ref[i], level)
                    one, two = jnp.exp2(max_ref[i] - joint), jnp.exp2(level - joint)
                    part = p_recv[slot, i * rows : (i + 1) * rows, :].astype(jnp.float32)
                    acc_ref[i] = acc_ref[i] * one + part * two
                    tot_ref[i] = tot_ref[i] * one + two
                    max_ref[i] = joint

    for i in range(half):
        out_ref[:, i * group : (i + 1) * group, :] = (
            (acc_ref[i] / tot_ref[i]).astype(jnp.bfloat16).reshape(requests, group, width)
        )

    for copy in kv_copies:
        copy.wait_send()

    for i in range(half):
        @pl.when(me + 1 < blocks)
        def _():
            q_copy(q_part(q_ref, i), me, i, 0, me + 1).wait_send()

        @pl.when(me >= 1)
        def _():
            q_copy(q_part(q_ref, i), me, i, 1, me - 1).wait_send()

    @pl.loop(1, blocks)
    def _(step):
        for i in range(half):
            @pl.when((me - step >= 0) & (me + 1 < blocks))
            def _():
                slot = me - step
                q_copy(q_part(q_all.at[slot], i), slot, i, 0, me + 1).wait_send()

            @pl.when((me + step < blocks) & (me >= 1))
            def _():
                slot = me + step
                q_copy(q_part(q_all.at[slot], i), slot, i, 1, me - 1).wait_send()

        slot = lax.rem(me + step, blocks)
        for i in range(half):
            for copy in p_copies(slot, i, me):
                copy.wait_send()


def local(queries, root_keys, root_values, branch_keys, branch_values, request_branch, seen_tokens):
    requests, heads, width = queries.shape
    root_tokens, shared, _ = root_keys.shape
    branches, per_branch, _, _ = branch_keys.shape
    branch_tokens = branches * per_branch
    blocks = lax.axis_size("blk")
    half = shared // lax.axis_size("pair")
    rows = requests * (heads // half)
    span = min(512, root_tokens, branch_tokens)
    bf16, f32 = jnp.bfloat16, jnp.float32
    dma = pltpu.SemaphoreType.DMA
    return pl.pallas_call(
        functools.partial(kernel, blocks, branches),
        out_shape=jax.ShapeDtypeStruct(queries.shape, bf16),
        in_specs=[pl.BlockSpec(memory_space=pltpu.VMEM)]
        + [pl.BlockSpec(memory_space=pl.ANY)] * 4
        + [pl.BlockSpec(memory_space=pltpu.SMEM)] * 2,
        out_specs=pl.BlockSpec(memory_space=pltpu.VMEM),
        scratch_shapes=[
            pltpu.VMEM((2, root_tokens * shared, width), bf16),
            pltpu.VMEM((2, branch_tokens * shared, width), bf16),
            pltpu.VMEM((span * shared, width), f32),
            pltpu.VMEM((2, half, 2 * root_tokens, width), bf16),
            pltpu.VMEM((2, half, 2 * branch_tokens, width), bf16),
            pltpu.VMEM((2, half, root_tokens, width), bf16),
            pltpu.VMEM((2, half, branch_tokens, width), bf16),
            pltpu.VMEM((blocks, requests, heads, width), bf16),
            pltpu.VMEM((blocks, half * rows, width), bf16),
            pltpu.VMEM((blocks, half * rows, width), bf16),
            pltpu.VMEM((blocks, half, 1, rows), f32),
            pltpu.VMEM((blocks, half, 1, rows), f32),
            pltpu.VMEM((half, rows, width), f32),
            pltpu.VMEM((half, rows, width), f32),
            pltpu.VMEM((half, rows, width), f32),
            dma((4,)),
            dma((4,)),
            dma((4,)),
            dma((2, blocks, half)),
            dma((blocks, half)),
            dma((blocks, half)),
            dma((blocks, half)),
            dma((blocks, half)),
            dma((blocks, half)),
        ],
        compiler_params=pltpu.CompilerParams(collective_id=0, has_side_effects=True),
        name="tree_attention",
    )(
        queries,
        root_keys.reshape(root_tokens * shared, width),
        root_values.reshape(root_tokens * shared, width),
        branch_keys.reshape(branch_tokens * shared, width),
        branch_values.reshape(branch_tokens * shared, width),
        request_branch,
        seen_tokens,
    )


def solution(mesh):
    in_specs = (
        P(("groups", "blk"), ("kv", "pair"), None),
        P(("groups", "blk", "pair"), "kv", None),
        P(("groups", "blk", "pair"), "kv", None),
        P(("groups", "blk"), "pair", "kv", None),
        P(("groups", "blk"), "pair", "kv", None),
        P(("groups", "blk")),
        P(("groups", "blk")),
    )
    out_specs = P(("groups", "blk"), ("kv", "pair"), None)
    return jax.shard_map(local, mesh=mesh, in_specs=in_specs, out_specs=out_specs, check_vma=False)
```

```python
import functools
import math

import jax
import jax.numpy as jnp
from jax import lax
from jax.experimental import pallas as pl
from jax.experimental.pallas import tpu as pltpu
from jax.sharding import PartitionSpec as P

MESH = pl.DeviceIdType.MESH
masked_floor = -1e30
log2e = 1.4426950408889634


def kernel(
    blocks, branches,
    q_ref, rk_ref, rv_ref, bk_ref, bv_ref, rb_ref, seen_ref,
    out_ref,
    in_r, in_b, stage, mine_r, mine_b, give_r, give_b,
    q_all, p_send, p_recv, s_send, s_recv, acc_ref, max_ref, tot_ref,
    load_sem, kv_send, kv_recv, q_send, q_recv, ps_sem, pr_sem, ss_sem, sr_sem,
):
    requests, heads, width = q_ref.shape
    half = mine_r.shape[1]
    shared = 2 * half
    group = heads // half
    rows = requests * group
    root_tokens = give_r.shape[2]
    branch_tokens = give_b.shape[2]
    per_branch = branch_tokens // branches
    factor = log2e / math.sqrt(width)
    me = lax.axis_index("blk")
    core = lax.axis_index("pair")
    other = 1 - core
    lower = 1 - (2 * me) // blocks

    loads = []
    for at, (src, dst) in enumerate(
        ((rk_ref, in_r.at[0]), (rv_ref, in_r.at[1]), (bk_ref, in_b.at[0]), (bv_ref, in_b.at[1]))
    ):
        copy = pltpu.make_async_copy(src, dst, load_sem.at[at])
        copy.start()
        loads.append(copy)

    barrier = pltpu.get_barrier_semaphore()

    for near in (me - 1, me + 1):
        @pl.when((near >= 0) & (near < blocks))
        def _():
            pl.semaphore_signal(barrier, inc=1, device_id={"blk": near}, device_id_type=MESH)

    pl.semaphore_signal(barrier, inc=1, device_id={"pair": other}, device_id_type=MESH)

    def q_part(ref, i):
        return ref.at[:, pl.ds(i * group, group), :]

    def q_copy(src, slot, i, side, target):
        return pltpu.make_async_remote_copy(
            src_ref=src,
            dst_ref=q_part(q_all.at[slot], i),
            send_sem=q_send.at[side, slot, i],
            recv_sem=q_recv.at[slot, i],
            device_id={"blk": target},
            device_id_type=MESH,
        )

    def forward(step):
        for i in range(half):
            @pl.when((me - step >= 0) & (me + 1 < blocks))
            def _():
                slot = me - step
                q_copy(q_part(q_ref, i), slot, i, 0, me).wait_recv()
                q_copy(q_part(q_all.at[slot], i), slot, i, 0, me + 1).start()

            @pl.when((me + step < blocks) & (me >= 1))
            def _():
                slot = me + step
                q_copy(q_part(q_ref, i), slot, i, 1, me).wait_recv()
                q_copy(q_part(q_all.at[slot], i), slot, i, 1, me - 1).start()

    def kv_copy(at, give, mine, kind, tokens):
        return pltpu.make_async_remote_copy(
            src_ref=give.at[kind],
            dst_ref=mine.at[kind, :, pl.ds(tokens, tokens), :],
            send_sem=kv_send.at[at],
            recv_sem=kv_recv.at[at],
            device_id={"pair": other},
            device_id_type=MESH,
        )

    kv_copies = (
        kv_copy(0, give_r, mine_r, 0, root_tokens),
        kv_copy(1, give_r, mine_r, 1, root_tokens),
        kv_copy(2, give_b, mine_b, 0, branch_tokens),
        kv_copy(3, give_b, mine_b, 1, branch_tokens),
    )
    span = stage.shape[0] // shared

    def spread(src, kind, mine, give, tokens):
        @pl.loop(0, tokens // span)
        def _(chunk):
            first = pl.multiple_of(chunk * (span * shared), span * shared)
            stage[...] = src[kind, pl.ds(first, span * shared), :].astype(jnp.float32)
            at = pl.multiple_of(chunk * span, span)
            for i in range(half):
                give[kind, i, pl.ds(at, span), :] = stage[
                    pl.ds(other * half + i, span, stride=shared), :
                ].astype(jnp.bfloat16)
                mine[kind, i, pl.ds(at, span), :] = stage[
                    pl.ds(core * half + i, span, stride=shared), :
                ].astype(jnp.bfloat16)

    @pl.when((me >= 1) & (me + 1 < blocks))
    def _():
        pl.semaphore_wait(barrier, 3)

    @pl.when((me < 1) | (me + 1 >= blocks))
    def _():
        pl.semaphore_wait(barrier, 2)

    for i in range(half):
        @pl.when(me + 1 < blocks)
        def _():
            q_copy(q_part(q_ref, i), me, i, 0, me + 1).start()

        @pl.when(me >= 1)
        def _():
            q_copy(q_part(q_ref, i), me, i, 1, me - 1).start()

    for kind in range(2):
        loads[kind].wait()
        spread(in_r, kind, mine_r, give_r, root_tokens)
        kv_copies[kind].start()

    for kind in range(2):
        loads[2 + kind].wait()
        spread(in_b, kind, mine_b, give_b, branch_tokens)
        kv_copies[2 + kind].start()
    forward(1)

    def attend(query, keys, values, ranges):
        scores = lax.dot_general(
            query, keys, (((1,), (1,)), ((), ())), preferred_element_type=jnp.float32
        )
        if ranges is not None:
            column = lax.broadcasted_iota(jnp.int32, (group, scores.shape[1]), 1)
            visible = [(column >= low) & (column < high) for low, high in ranges]
            scores = jnp.concatenate(
                [
                    jnp.where(seen, scores[r * group : (r + 1) * group], masked_floor)
                    for r, seen in enumerate(visible)
                ],
                axis=0,
            )
        largest = jnp.max(scores, axis=-1, keepdims=True)
        weights = jnp.exp2((scores - largest) * factor)
        if ranges is not None:
            weights = jnp.where(scores > 0.5 * masked_floor, weights, 0.0)
        totals = jnp.sum(weights, axis=-1, keepdims=True)
        sums = jnp.dot(weights.astype(jnp.bfloat16), values, preferred_element_type=jnp.float32)
        return sums, largest * factor, totals

    def p_copies(slot, i, target):
        place = pl.ds(i * rows, rows)
        return (
            pltpu.make_async_remote_copy(
                src_ref=p_send.at[slot, place, :],
                dst_ref=p_recv.at[target, place, :],
                send_sem=ps_sem.at[slot, i],
                recv_sem=pr_sem.at[target, i],
                device_id={"blk": slot},
                device_id_type=MESH,
            ),
            pltpu.make_async_remote_copy(
                src_ref=s_send.at[slot, i],
                dst_ref=s_recv.at[target, i],
                send_sem=ss_sem.at[slot, i],
                recv_sem=sr_sem.at[target, i],
                device_id={"blk": slot},
                device_id_type=MESH,
            ),
        )

    kv_copies[0].wait_recv()
    kv_copies[1].wait_recv()

    @pl.loop(1, blocks)
    def _(step):
        @pl.loop(0, 2)
        def _(turn):
            side = turn + lower * (1 - 2 * turn)
            slot = me + step * (2 * side - 1)
            after = me + 1 - 2 * side

            @pl.when((turn == 1) & (step + 1 < blocks))
            def _():
                forward(step + 1)

            @pl.when((slot >= 0) & (slot < blocks))
            def _():
                for i in range(half):
                    @pl.when((after < 0) | (after >= blocks))
                    def _():
                        q_copy(q_part(q_ref, i), slot, i, 0, me).wait_recv()

                    query = q_all[slot, :, i * group : (i + 1) * group, :].reshape(rows, width)
                    sums, largest, totals = attend(query, mine_r[0, i], mine_r[1, i], None)
                    p_send[slot, i * rows : (i + 1) * rows, :] = (sums / totals).astype(
                        jnp.bfloat16
                    )
                    level = jnp.broadcast_to(largest + jnp.log(totals) * log2e, (rows, 128))
                    s_send[slot, i] = level.T[0:1, :]
                    for copy in p_copies(slot, i, me):
                        copy.start()

    kv_copies[2].wait_recv()
    kv_copies[3].wait_recv()
    ranges = ([], [])
    for r in range(requests):
        start = lax.rem(rb_ref[r], branches) * per_branch
        seen = seen_ref[r]
        for piece, owner in enumerate((core, other)):
            length = jnp.clip(seen - owner * per_branch, 0, per_branch)
            ranges[piece].append((start, start + length))
    for i in range(half):
        query = q_ref[:, i * group : (i + 1) * group, :].reshape(rows, width)
        sums, largest, totals = attend(query, mine_r[0, i], mine_r[1, i], None)
        for piece in range(2):
            place = slice(piece * branch_tokens, (piece + 1) * branch_tokens)
            more = attend(query, mine_b[0, i, place, :], mine_b[1, i, place, :], ranges[piece])
            joint = jnp.maximum(largest, more[1])
            one, two = jnp.exp2(largest - joint), jnp.exp2(more[1] - joint)
            sums = sums * one + more[0] * two
            totals = totals * one + more[2] * two
            largest = joint
        acc_ref[i] = sums
        max_ref[i] = jnp.broadcast_to(largest, (rows, width))
        tot_ref[i] = jnp.broadcast_to(totals, (rows, width))

    @pl.loop(1, blocks)
    def _(step):
        @pl.loop(0, 2)
        def _(side):
            slot = me + step * (2 * side - 1)

            @pl.when((slot >= 0) & (slot < blocks))
            def _():
                for i in range(half):
                    for copy in p_copies(slot, i, slot):
                        copy.wait_recv()
                    level = jnp.broadcast_to(s_recv[slot, i], (128, rows)).T
                    joint = jnp.maximum(max_ref[i], level)
                    one, two = jnp.exp2(max_ref[i] - joint), jnp.exp2(level - joint)
                    part = p_recv[slot, i * rows : (i + 1) * rows, :].astype(jnp.float32)
                    acc_ref[i] = acc_ref[i] * one + part * two
                    tot_ref[i] = tot_ref[i] * one + two
                    max_ref[i] = joint

    for i in range(half):
        out_ref[:, i * group : (i + 1) * group, :] = (
            (acc_ref[i] / tot_ref[i]).astype(jnp.bfloat16).reshape(requests, group, width)
        )

    for copy in kv_copies:
        copy.wait_send()

    for i in range(half):
        @pl.when(me + 1 < blocks)
        def _():
            q_copy(q_part(q_ref, i), me, i, 0, me + 1).wait_send()

        @pl.when(me >= 1)
        def _():
            q_copy(q_part(q_ref, i), me, i, 1, me - 1).wait_send()

    @pl.loop(1, blocks)
    def _(step):
        for i in range(half):
            @pl.when((me - step >= 0) & (me + 1 < blocks))
            def _():
                slot = me - step
                q_copy(q_part(q_all.at[slot], i), slot, i, 0, me + 1).wait_send()

            @pl.when((me + step < blocks) & (me >= 1))
            def _():
                slot = me + step
                q_copy(q_part(q_all.at[slot], i), slot, i, 1, me - 1).wait_send()

        slot = lax.rem(me + step, blocks)
        for i in range(half):
            for copy in p_copies(slot, i, me):
                copy.wait_send()


def local(queries, root_keys, root_values, branch_keys, branch_values, request_branch, seen_tokens):
    requests, heads, width = queries.shape
    root_tokens, shared, _ = root_keys.shape
    branches, per_branch, _, _ = branch_keys.shape
    branch_tokens = branches * per_branch
    blocks = lax.axis_size("blk")
    half = shared // lax.axis_size("pair")
    rows = requests * (heads // half)
    span = min(512, root_tokens, branch_tokens)
    bf16, f32 = jnp.bfloat16, jnp.float32
    dma = pltpu.SemaphoreType.DMA
    return pl.pallas_call(
        functools.partial(kernel, blocks, branches),
        out_shape=jax.ShapeDtypeStruct(queries.shape, bf16),
        in_specs=[pl.BlockSpec(memory_space=pltpu.VMEM)]
        + [pl.BlockSpec(memory_space=pl.ANY)] * 4
        + [pl.BlockSpec(memory_space=pltpu.SMEM)] * 2,
        out_specs=pl.BlockSpec(memory_space=pltpu.VMEM),
        scratch_shapes=[
            pltpu.VMEM((2, root_tokens * shared, width), bf16),
            pltpu.VMEM((2, branch_tokens * shared, width), bf16),
            pltpu.VMEM((span * shared, width), f32),
            pltpu.VMEM((2, half, 2 * root_tokens, width), bf16),
            pltpu.VMEM((2, half, 2 * branch_tokens, width), bf16),
            pltpu.VMEM((2, half, root_tokens, width), bf16),
            pltpu.VMEM((2, half, branch_tokens, width), bf16),
            pltpu.VMEM((blocks, requests, heads, width), bf16),
            pltpu.VMEM((blocks, half * rows, width), bf16),
            pltpu.VMEM((blocks, half * rows, width), bf16),
            pltpu.VMEM((blocks, half, 1, rows), f32),
            pltpu.VMEM((blocks, half, 1, rows), f32),
            pltpu.VMEM((half, rows, width), f32),
            pltpu.VMEM((half, rows, width), f32),
            pltpu.VMEM((half, rows, width), f32),
            dma((4,)),
            dma((4,)),
            dma((4,)),
            dma((2, blocks, half)),
            dma((blocks, half)),
            dma((blocks, half)),
            dma((blocks, half)),
            dma((blocks, half)),
            dma((blocks, half)),
        ],
        compiler_params=pltpu.CompilerParams(collective_id=0, has_side_effects=True),
        name="tree_attention",
    )(
        queries,
        root_keys.reshape(root_tokens * shared, width),
        root_values.reshape(root_tokens * shared, width),
        branch_keys.reshape(branch_tokens * shared, width),
        branch_values.reshape(branch_tokens * shared, width),
        request_branch,
        seen_tokens,
    )


def solution(mesh):
    in_specs = (
        P(("groups", "blk"), ("kv", "pair"), None),
        P(("groups", "blk", "pair"), "kv", None),
        P(("groups", "blk", "pair"), "kv", None),
        P(("groups", "blk"), "pair", "kv", None),
        P(("groups", "blk"), "pair", "kv", None),
        P(("groups", "blk")),
        P(("groups", "blk")),
    )
    out_specs = P(("groups", "blk"), ("kv", "pair"), None)
    return jax.shard_map(local, mesh=mesh, in_specs=in_specs, out_specs=out_specs, check_vma=False)
```
